256 devices in a mesh: head: 32 (over y, z), dp: 8 (over x, core).
Axes of the slice: x: 4, y: 4, z: 8, core: 2. Of those that a mesh axis runs over, the one named last changes fastest.
Arguments:
- attn_out: bfloat16 [2048, 8192], P('dp', 'head'), may hold values from -6 to 6
- head_mask: int32 [64], P('head'), may hold values from 0 to 1, as said below
- gate_scale: float32 [64], P('head'), may hold values from 0.25 to 2
- w_out: bfloat16 [8192, 8192], P('head', 'dp'), may hold values from -0.09375 to 0.09375
- grad_out: bfloat16 [2048, 8192], P(('dp', 'head')), may hold values from -6 to 6
Outputs:
- proj_out: bfloat16 [2048, 8192], P(('dp', 'head'))
- grad_attn: bfloat16 [2048, 8192], P('dp', 'head')
- grad_w: float32 [8192, 8192], P('head', 'dp')
The draws below stay inside these ranges and needn't reach their ends.
Inputs may be any that keep to these rules, and one draw needn't show every extreme that they name: `head_mask`: exactly 32 heads are live.
All inputs are finite; a program needn't handle non-finite values.
Results may differ from the reference program's by a relative error of at most 0.0051.
Values may be sent and summed in bfloat16 or wider, within the bound.
No kernel may reach another device: no remote copies, remote signals or barrier semaphores. Data moves between devices by JAX's collectives and lax.ppermute only.
A program may use at most 128 MiB of HBM per device.

```python
import math
import jax
import jax.numpy as jnp
from jax import lax

D = 8192
HEADS = 64
HEAD_DIM = 128
TOKENS = 2048


def draw_head_mask(key, part):
    order = jax.random.permutation(key, HEADS)
    return (order < HEADS // 2).astype(jnp.int32)


def block_levels(rng, extent, shards, low, largest):
    level, own = 1.0, jax.random.fold_in(rng, 6)
    for axis_at, shards_of in shards:
        steps = jnp.exp(jax.random.uniform(jax.random.fold_in(own, axis_at), (shards_of,), jnp.float32, low / len(shards), largest / len(shards)))
        level = level * jnp.repeat(steps, extent[axis_at] // shards_of).reshape([-1 if axis == axis_at else 1 for axis in range(len(extent))])
    return level


def gaussian(rng, extent, scale, most, split=(), dtype=jnp.bfloat16):
    entries = scale * jax.random.normal(rng, extent, jnp.float32)
    if split:
        entries = entries * block_levels(rng, extent, split, -0.22, 0.18)
    return jnp.clip(entries, -most, most).astype(dtype)


def setup_inputs(seed: int = 0) -> dict:
    keys = jax.random.split(jax.random.key(seed), 6)
    return {
        "attn_out": gaussian(keys[0], (TOKENS, HEADS * HEAD_DIM), 1.0, 6.0, ((0, 8), (1, 32))),
        "head_mask": draw_head_mask(jax.random.fold_in(keys[5], 71), 0),
        "gate_scale": jnp.clip(jnp.exp(math.log(2.0) - 2.0794415 * jax.random.uniform(keys[2], (HEADS,), jnp.float32) ** block_levels(keys[2], (HEADS,), ((0, 32),), -0.2, 0.2)), 0.25, 2.0),
        "w_out": gaussian(keys[3], (HEADS * HEAD_DIM, D), (HEADS * HEAD_DIM // 2) ** -0.5, 0.09375, ((0, 32), (1, 8))),
        "grad_out": gaussian(keys[4], (TOKENS, D), 1.0, 6.0, ((0, 256),)),
    }


def reference(attn_out, head_mask, gate_scale, w_out, grad_out):
    gate_vals = head_mask.astype(jnp.float32) * gate_scale
    col_gate = jnp.repeat(gate_vals, HEAD_DIM)
    gated = (attn_out.astype(jnp.float32) * col_gate[None, :]).astype(jnp.bfloat16)
    proj_out = jnp.dot(gated, w_out, preferred_element_type=jnp.float32).astype(jnp.bfloat16)
    back_proj = lax.dot_general(grad_out, w_out, (((1,), (1,)), ((), ())), preferred_element_type=jnp.float32)
    grad_attn = (back_proj * col_gate[None, :]).astype(jnp.bfloat16)
    grad_w = lax.dot_general(gated, grad_out, (((0,), (0,)), ((), ())), preferred_element_type=jnp.float32)
    return proj_out, grad_attn, grad_w
```

```python
import jax
import jax.numpy as jnp
from jax import lax
from jax.sharding import Mesh, PartitionSpec as P

BF = jnp.bfloat16
F32 = jnp.float32


def exchange(v, axes):
    return lax.all_to_all(v, axes, split_axis=0, concat_axis=0, tiled=False)


def shards(attn_out, head_mask, gate_scale, w_out, grad_out):
    nx, ny, nz, nc = (lax.axis_size(a) for a in "xyzc")
    core = lax.axis_index("c")
    swap = [(0, 1), (1, 0)]
    t, r = attn_out.shape
    j, d = grad_out.shape
    q = d // (nx * nc * ny)
    gate_vals = head_mask.astype(F32) * gate_scale
    col_gate = jnp.repeat(gate_vals, r // gate_vals.shape[0])
    gated = (attn_out.astype(F32) * col_gate[None, :]).astype(BF)

    a_all = lax.all_gather(gated, ("x", "y"), axis=0, tiled=False)
    a_all = a_all.reshape(nx, ny, t, r)

    g5 = grad_out.reshape(j, nx, nc, ny, q)
    g5 = jnp.where(core == 0, g5, g5[:, :, ::-1])
    g_send = g5.transpose(1, 3, 0, 2, 4).reshape(nx * ny, j, nc * q)
    g_mine = exchange(g_send, ("x", "y"))
    g_mine = jnp.broadcast_to(g_mine[None], (nz,) + g_mine.shape)
    g_all = exchange(g_mine, "z")
    g_all = g_all.transpose(1, 0, 2, 3).reshape(nx * t, nc * q)

    w_send = w_out.reshape(r, ny, q).transpose(1, 0, 2)
    w_mine = exchange(w_send, "y")
    w_other = lax.ppermute(w_mine, "c", swap)
    w_all = jnp.concatenate([w_mine, w_other], axis=2).reshape(ny * r, nc * q)

    a_mat = a_all.transpose(0, 2, 1, 3).reshape(nx * t, ny * r)
    part = jnp.dot(a_mat, w_all, preferred_element_type=F32).astype(BF)
    part = part.reshape(nx * ny, nz, j, nc * q).transpose(1, 0, 2, 3)
    proj = exchange(part, "z").astype(F32).sum(axis=0).astype(BF)
    proj = exchange(proj, ("x", "y")).reshape(nx, ny, j, nc, q)
    proj = proj.transpose(2, 0, 3, 1, 4)
    proj = jnp.where(core == 0, proj, proj[:, :, ::-1])
    proj_out = proj.reshape(j, d)

    back = lax.dot_general(g_all, w_all, (((1,), (1,)), ((), ())), preferred_element_type=F32)
    back = back.astype(BF).reshape(nx, t, ny, r).transpose(0, 2, 1, 3).reshape(nx * ny, t, r)
    back = exchange(back, ("x", "y")).astype(F32).sum(axis=0)
    grad_attn = (back * col_gate[None, :]).astype(BF)

    gw = lax.dot_general(a_mat, g_all, (((0,), (0,)), ((), ())), preferred_element_type=F32)
    gw = gw.reshape(ny, r, nc, q)
    gw = gw[:, :, 0] + lax.ppermute(gw[:, :, 1], "c", swap)
    gw = exchange(gw, "y")
    grad_w = gw.transpose(1, 0, 2).reshape(r, ny * q)
    return (proj_out, grad_attn, grad_w)


def solution(mesh):
    fine = Mesh(mesh.devices.reshape(4, 8, 4, 2), ("y", "z", "x", "c"))
    dp, head = ("x", "c"), ("y", "z")
    return jax.shard_map(
        shards,
        mesh=fine,
        in_specs=(P(dp, head), P(head), P(head), P(head, dp), P(dp + head, None)),
        out_specs=(P(dp + head, None), P(dp, head), P(head, dp)),
        check_vma=False,
    )
```

```python
import jax
import jax.numpy as jnp
from jax import lax
from jax.sharding import Mesh, PartitionSpec as P

BF = jnp.bfloat16
F32 = jnp.float32


def exchange(v, axes):
    return lax.all_to_all(v, axes, split_axis=0, concat_axis=0, tiled=False)


def exchange_y(v):
    n = v.shape[0]
    me = lax.axis_index("y")
    got = [lax.dynamic_index_in_dim(v, me, 0, keepdims=False)]
    for s in range(1, n):
        piece = lax.dynamic_index_in_dim(v, (me + s) % n, 0, keepdims=False)
        got.append(lax.ppermute(piece, "y", [(i, (i + s) % n) for i in range(n)]))
    ring = jnp.stack([got[(n - 1 - k) % n] for k in range(2 * n - 1)])
    return lax.dynamic_slice_in_dim(ring, n - 1 - me, n, 0)


def shards(attn_out, head_mask, gate_scale, w_out, grad_out):
    nx, ny, nz, nc = (lax.axis_size(a) for a in "xyzc")
    core = lax.axis_index("c")
    swap = [(0, 1), (1, 0)]
    t, r = attn_out.shape
    j, d = grad_out.shape
    q = d // (nx * nc * ny)
    gate_vals = head_mask.astype(F32) * gate_scale
    col_gate = jnp.repeat(gate_vals, r // gate_vals.shape[0])
    gated = (attn_out.astype(F32) * col_gate[None, :]).astype(BF)
    gated = gated.reshape(ny, nz, j, r).transpose(1, 0, 2, 3)
    gated, grad_out = lax.optimization_barrier((gated, grad_out))

    a_all = lax.all_gather(gated.reshape(t, r), ("x", "y"), axis=0, tiled=True)

    g5 = grad_out.reshape(j, nx, nc, ny, q)
    g5 = jnp.where(core == 0, g5, g5[:, :, ::-1])
    g_send = g5.transpose(1, 3, 0, 2, 4).reshape(nx * ny, j, nc * q)
    g_mine = exchange(g_send, ("x", "y"))
    g_mine = jnp.broadcast_to(g_mine[None], (nz,) + g_mine.shape)
    g_all = exchange(g_mine, "z").reshape(nx * t, nc * q)

    w_mine = exchange_y(w_out.reshape(r, ny, q).transpose(1, 0, 2))
    w_other = lax.ppermute(w_mine, "c", swap)
    w_all = jnp.concatenate([w_mine, w_other], axis=2).reshape(ny * r, nc * q)

    a_all, g_all, w_all = lax.optimization_barrier((a_all, g_all, w_all))
    a_mat = a_all.reshape(nx, ny, nz, ny * j, r).transpose(2, 0, 3, 1, 4).reshape(nx * t, ny * r)
    part = jnp.dot(a_mat, w_all, preferred_element_type=F32)
    proj = lax.psum_scatter(part, "z", scatter_dimension=0, tiled=True).astype(BF)
    proj = exchange(proj.reshape(nx * ny, j, nc * q), ("x", "y")).reshape(nx, ny, j, nc, q)
    proj = proj.transpose(2, 0, 3, 1, 4)
    proj = jnp.where(core == 0, proj, proj[:, :, ::-1])
    proj_out = proj.reshape(j, d)

    part, g_all = lax.optimization_barrier((part, g_all))
    back = lax.dot_general(g_all, w_all, (((1,), (1,)), ((), ())), preferred_element_type=F32)
    back = back.astype(BF).reshape(nz, nx, ny * j, ny, r).transpose(1, 3, 0, 2, 4)
    back = exchange(back.reshape(nx * ny, t, r), ("x", "y")).astype(F32).sum(axis=0)
    back = back.reshape(nz, ny, j, r).transpose(1, 0, 2, 3).reshape(t, r)
    grad_attn = (back * col_gate[None, :]).astype(BF)

    gw = lax.dot_general(a_mat, g_all, (((0,), (0,)), ((), ())), preferred_element_type=F32)
    gw = gw.reshape(ny, r, nc, q)
    gw = gw[:, :, 0] + lax.ppermute(gw[:, :, 1], "c", swap)
    gw = exchange_y(gw)
    grad_w = gw.transpose(1, 0, 2).reshape(r, ny * q)
    return (proj_out, grad_attn, grad_w)


def solution(mesh):
    fine = Mesh(mesh.devices.reshape(4, 8, 4, 2), ("y", "z", "x", "c"))
    dp, head = ("x", "c"), ("y", "z")
    return jax.shard_map(
        shards,
        mesh=fine,
        in_specs=(P(dp, head), P(head), P(head), P(head, dp), P(dp + head, None)),
        out_specs=(P(dp + head, None), P(dp, head), P(head, dp)),
        check_vma=False,
    )
```

```python
import jax
import jax.numpy as jnp
from jax import lax
from jax.sharding import Mesh, PartitionSpec as P

BF = jnp.bfloat16
F32 = jnp.float32
XC = ("x", "c")


def exchange(v, axes):
    return lax.all_to_all(v, axes, split_axis=0, concat_axis=0, tiled=False)


def shift_y(v, s):
    n = lax.axis_size("y")
    return lax.ppermute(v, "y", [(i, (i + s) % n) for i in range(n)])


def shards(attn_out, head_mask, gate_scale, w_out, grad_out):
    ny, nz = lax.axis_size("y"), lax.axis_size("z")
    nxc = lax.axis_size("x") * lax.axis_size("c")
    me = lax.axis_index("y")
    t, r = attn_out.shape
    j, d = grad_out.shape
    n = d // nxc
    ty = t // ny
    gate_vals = head_mask.astype(F32) * gate_scale
    col_gate = jnp.repeat(gate_vals, r // gate_vals.shape[0])
    gated = (attn_out.astype(F32) * col_gate[None, :]).astype(BF).reshape(ny, ty, r)

    a_y = [lax.dynamic_index_in_dim(gated, (me + s) % ny, 0, keepdims=False) for s in range(ny)]
    a_y = [a_y[0]] + [shift_y(a_y[s], s) for s in range(1, ny)]
    a_y = jnp.concatenate(a_y, axis=1)
    a_all = lax.all_gather(a_y, XC, axis=0, tiled=True)

    w_all = [w_out] + [shift_y(w_out, s) for s in range(1, ny)]

    g = exchange(grad_out.reshape(j, nxc, n).transpose(1, 0, 2), XC)
    g = exchange(jnp.broadcast_to(g[None], (nz,) + g.shape), "z")

    a_all, g, w_all = lax.optimization_barrier((a_all, g, w_all))
    w = jnp.concatenate(w_all, axis=0)
    a = a_all.reshape(nxc, nz, j, ny * r).transpose(1, 0, 2, 3).reshape(nxc * nz * j, ny * r)
    g = g.reshape(nxc * nz * j, n)

    part = jnp.dot(a, w, preferred_element_type=F32).astype(BF)
    proj = exchange(part.reshape(nz, nxc, j, n), "z").astype(F32).sum(axis=0).astype(BF)
    proj = exchange(proj, XC)
    proj_out = proj.transpose(1, 0, 2).reshape(j, d)

    part, g = lax.optimization_barrier((part, g))
    back = lax.dot_general(g, w, (((1,), (1,)), ((), ())), preferred_element_type=F32)
    back = back.reshape(nz, nxc, j, ny * r).transpose(1, 0, 2, 3).reshape(nxc * ty, ny * r)
    back, g = lax.optimization_barrier((back, g))
    mine = lax.psum_scatter(back, XC, scatter_dimension=0, tiled=True)
    mine = [mine[:, s * r : (s + 1) * r] for s in range(ny)]
    mine = [mine[0]] + [shift_y(mine[s], -s) for s in range(1, ny)]
    ring = jnp.stack(mine + mine[:-1])
    mine = lax.dynamic_slice_in_dim(ring, (ny - me) % ny, ny, 0).reshape(t, r)
    grad_attn = (mine * col_gate[None, :]).astype(BF)

    gw = lax.dot_general(a, g, (((0,), (0,)), ((), ())), preferred_element_type=F32)
    gw = gw.reshape(ny, r, n)
    grad_w = gw[0]
    for s in range(1, ny):
        grad_w = grad_w + shift_y(gw[s].astype(BF), -s).astype(F32)
    return (proj_out, grad_attn, grad_w)


def solution(mesh):
    fine = Mesh(mesh.devices.reshape(4, 8, 4, 2), ("y", "z", "x", "c"))
    dp, head = XC, ("y", "z")
    return jax.shard_map(
        shards,
        mesh=fine,
        in_specs=(P(dp, head), P(head), P(head), P(head, dp), P(dp + head, None)),
        out_specs=(P(dp + head, None), P(dp, head), P(head, dp)),
        check_vma=False,
    )
```

```python
import jax
import jax.numpy as jnp
from jax import lax
from jax.sharding import Mesh, PartitionSpec as P

BF = jnp.bfloat16
F32 = jnp.float32
XC = ("x", "c")


def exchange(v, axes):
    return lax.all_to_all(v, axes, split_axis=0, concat_axis=0, tiled=False)


def shift(v, axis, s):
    n = lax.axis_size(axis)
    return lax.ppermute(v, axis, [(i, (i + s) % n) for i in range(n)])


def relative(v):
    nx = v.shape[0]
    ring = jnp.concatenate([v[::-1], v[::-1]])
    v = lax.dynamic_slice_in_dim(ring, nx - 1 - lax.axis_index("x"), nx, 0)
    return jnp.where(lax.axis_index("c") == 0, v, v[:, ::-1])


def shards(attn_out, head_mask, gate_scale, w_out, grad_out):
    nx, ny, nz, nc = (lax.axis_size(a) for a in "xyzc")
    me = lax.axis_index("y")
    t, r = attn_out.shape
    j, d = grad_out.shape
    n = d // (nx * nc)
    ty = t // ny
    half = r // 2

    g = exchange(grad_out.reshape(j, nx * nc, n).transpose(1, 0, 2), XC)
    g = relative(g.reshape(nx, nc, j, n)).transpose(1, 0, 2, 3)

    gate_vals = head_mask.astype(F32) * gate_scale
    col_gate = jnp.repeat(gate_vals, r // gate_vals.shape[0])
    gated = (attn_out.astype(F32) * col_gate[None, :]).astype(BF).reshape(ny, ty, r)

    a = [lax.dynamic_index_in_dim(gated, (me + s) % ny, 0, keepdims=False) for s in range(ny)]
    a = [a[0]] + [shift(a[s], "y", s) for s in range(1, ny)]
    a = jnp.concatenate(a, axis=1)
    a, g = lax.optimization_barrier((a, g.reshape(nc * nx * j, n)))
    g = lax.all_gather(g, "z", axis=0, tiled=True)
    a = jnp.stack([a] + [shift(a, "x", s) for s in range(1, nx)])
    a = jnp.stack([a, shift(a, "c", 1)])

    w1, w3 = shift(w_out, "y", 1), shift(w_out, "y", -1)
    w2 = [shift(w1[:half], "y", 1), shift(w3[half:], "y", -1)]
    a, w = lax.optimization_barrier((a, [w_out, w1, *w2, w3]))
    w = jnp.concatenate(w, axis=0)
    a = a.reshape(nc * nx, nz, j, ny * r).transpose(1, 0, 2, 3).reshape(nx * nc * ty, ny * r)

    part = jnp.dot(a, w, preferred_element_type=F32).astype(BF)
    proj = exchange(part.reshape(nz, nc, nx, j, n), "z").astype(F32).sum(axis=0).astype(BF)
    proj = relative(proj.transpose(1, 0, 2, 3)).reshape(nx * nc, j, n)
    proj = exchange(proj, XC)
    proj_out = proj.transpose(1, 0, 2).reshape(j, d)

    back = lax.dot_general(g, w, (((1,), (1,)), ((), ())), preferred_element_type=F32)
    back = back.reshape(nz, nc, nx, j, ny * r).transpose(1, 2, 0, 3, 4)
    own = back[0] + shift(back[1].astype(BF), "c", 1).astype(F32)
    mine = own[0]
    for s in range(1, nx):
        mine = mine + shift(own[s].astype(BF), "x", -s).astype(F32)
    mine = mine.reshape(ty, ny * r)
    mine = [mine[:, s * r : (s + 1) * r] for s in range(ny)]
    mine = [mine[0]] + [shift(mine[s], "y", -s) for s in range(1, ny)]
    ring = jnp.stack(mine + mine[:-1])
    mine = lax.dynamic_slice_in_dim(ring, (ny - me) % ny, ny, 0).reshape(t, r)
    grad_attn = (mine * col_gate[None, :]).astype(BF)

    back, g = lax.optimization_barrier((back, g))
    gw = lax.dot_general(a, g, (((0,), (0,)), ((), ())), preferred_element_type=F32)
    gw = gw.reshape(ny, 2, half, n)
    near = gw[1].at[0].add(shift(gw[2, 0].astype(BF), "y", -1).astype(F32))
    far = gw[3].at[1].add(shift(gw[2, 1].astype(BF), "y", 1).astype(F32))
    near, far = shift(near.astype(BF), "y", -1), shift(far.astype(BF), "y", 1)
    grad_w = (gw[0] + near.astype(F32) + far.astype(F32)).reshape(r, n)
    return (proj_out, grad_attn, grad_w)


def solution(mesh):
    fine = Mesh(mesh.devices.reshape(4, 8, 4, 2), ("y", "z", "x", "c"))
    dp, head = XC, ("y", "z")
    return jax.shard_map(
        shards,
        mesh=fine,
        in_specs=(P(dp, head), P(head), P(head), P(head, dp), P(dp + head, None)),
        out_specs=(P(dp + head, None), P(dp, head), P(head, dp)),
        check_vma=False,
    )
```

```python
import jax
import jax.numpy as jnp
from jax import lax
from jax.experimental import pallas as pl
from jax.experimental.pallas import tpu as pltpu
from jax.sharding import Mesh, PartitionSpec as P

BF = jnp.bfloat16
F32 = jnp.float32
XC = ("x", "c")
FWD = 2**30
BWD = 2**36
VMEM = pl.BlockSpec(memory_space=pltpu.VMEM)
SMEM = pl.BlockSpec(memory_space=pltpu.SMEM)


def exchange(v, axes):
    return lax.all_to_all(v, axes, split_axis=0, concat_axis=0, tiled=False)


def shift(v, axis, s):
    n = lax.axis_size(axis)
    return lax.ppermute(v, axis, [(i, (i + s) % n) for i in range(n)])


def place(where, e, s, nx):
    return ((where[0] - s) & (nx - 1)) * 2 + (where[1] ^ e)


def forward(where, own, other, w0, w1, w2a, w2b, w3, out):
    nx, ty, _ = own.shape
    nz, _, j, n = out.shape
    r = w0.shape[0]
    half = r // 2
    for e, a in enumerate((own, other)):
        rows = a[...].reshape(nx * ty, a.shape[2])
        total = jnp.dot(rows[:, :r], w0[...], preferred_element_type=F32)
        total += jnp.dot(rows[:, r : 2 * r], w1[...], preferred_element_type=F32)
        total += jnp.dot(rows[:, 2 * r : 2 * r + half], w2a[...], preferred_element_type=F32)
        total += jnp.dot(rows[:, 2 * r + half : 3 * r], w2b[...], preferred_element_type=F32)
        total += jnp.dot(rows[:, 3 * r :], w3[...], preferred_element_type=F32)
        for s in range(nx):
            out[:, place(where, e, s, nx)] = total[s * ty : (s + 1) * ty].reshape(nz, j, n)


def backward(where, g, w0, w1, w2a, w2b, w3, out, g_rel, rows):
    nz, nxc, j, n = g.shape
    ny, ty, r = out.shape[1:]
    half = r // 2
    for k in range(nxc):
        rows[k * ty : (k + 1) * ty] = g[:, k].astype(F32).reshape(ty, n).astype(BF)
    for e in range(2):
        for s in range(nxc // 2):
            k = e * (nxc // 2) + s
            at = pl.multiple_of(place(where, e, s, nxc // 2) * ty, ty)
            g_rel[k * ty : (k + 1) * ty] = rows[pl.ds(at, ty)]
    across = (((1,), (1,)), ((), ()))
    for s, w in enumerate(((w0,), (w1,), (w2a, w2b), (w3,))):
        at = (where[2] - s) & (ny - 1)
        width = r // len(w)
        for i, part in enumerate(w):
            v = lax.dot_general(rows[...], part[...], across, preferred_element_type=F32)
            out[:, at, :, i * width : (i + 1) * width] = v.astype(BF).reshape(nxc, ty, width)


def call(kernel, out_shape, *args, scratch=(), flops):
    return pl.pallas_call(
        kernel,
        out_shape=out_shape,
        in_specs=[SMEM] + [VMEM] * (len(args) - 1),
        out_specs=jax.tree.map(lambda _: VMEM, out_shape),
        scratch_shapes=scratch,
        cost_estimate=pl.CostEstimate(flops=flops, bytes_accessed=flops // 400, transcendentals=0),
        compiler_params=pltpu.CompilerParams(vmem_limit_bytes=32 * 1024 * 1024),
    )(*args)


def shards(attn_out, head_mask, gate_scale, w_out, grad_out):
    nx, ny, nz, nc = (lax.axis_size(a) for a in "xyzc")
    me = lax.axis_index("y")
    where = jnp.stack([lax.axis_index("x"), lax.axis_index("c"), me]).astype(jnp.int32)
    t, r = attn_out.shape
    j, d = grad_out.shape
    n = d // (nx * nc)
    ty = t // ny
    half = r // 2

    w1, w3 = shift(w_out, "y", 1), shift(w_out, "y", -1)
    g = exchange(grad_out.reshape(j, nx * nc, n).transpose(1, 0, 2), XC)

    gate_vals = head_mask.astype(F32) * gate_scale
    col_gate = jnp.repeat(gate_vals, r // gate_vals.shape[0])
    gated = (attn_out.astype(F32) * col_gate[None, :]).astype(BF).reshape(ny, ty, r)

    a = [lax.dynamic_index_in_dim(gated, (me + s) % ny, 0, keepdims=False) for s in range(ny)]
    a = [a[0]] + [shift(a[s], "y", s) for s in range(1, ny)]
    a = jnp.concatenate(a, axis=1)
    a, g, w1, w3 = lax.optimization_barrier((a, g, w1, w3))
    g = exchange(jnp.broadcast_to(g[None], (nz,) + g.shape), "z")
    a = jnp.stack([a] + [shift(a, "x", s) for s in range(1, nx)])
    w2a, w2b = shift(w1[:half], "y", 1), shift(w3[half:], "y", -1)
    other = shift(a, "c", 1)
    w = (w_out, w1, w2a, w2b, w3)

    part = call(
        forward, jax.ShapeDtypeStruct((nz, nx * nc, j, n), F32), where, a, other, *w,
        flops=FWD,
    )
    proj = lax.psum_scatter(part, "z", scatter_dimension=0, tiled=False).astype(BF)
    proj = exchange(proj, XC)
    proj_out = proj.transpose(1, 0, 2).reshape(j, d)

    part, g = lax.optimization_barrier((part, g))
    back, g_rel = call(
        backward,
        (
            jax.ShapeDtypeStruct((nx * nc, ny, ty, r), BF),
            jax.ShapeDtypeStruct((nx * nc * ty, n), BF),
        ),
        where, g, *w,
        scratch=[pltpu.VMEM((nx * nc * ty, n), BF)],
        flops=BWD,
    )
    mine = exchange(back.reshape(nx * nc * ny, ty, r), ("x", "c", "y"))
    mine = mine.astype(F32).reshape(nx * nc, t, r).sum(axis=0)
    grad_attn = (mine * col_gate[None, :]).astype(BF)

    a_rel = jnp.concatenate([a, other]).reshape(nx * nc * ty, ny * r)
    gw = lax.dot_general(a_rel, g_rel, (((0,), (0,)), ((), ())), preferred_element_type=F32)
    gw = gw.reshape(ny, 2, half, n)
    near = gw[1].at[0].add(shift(gw[2, 0].astype(BF), "y", -1).astype(F32))
    far = gw[3].at[1].add(shift(gw[2, 1].astype(BF), "y", 1).astype(F32))
    near, far = shift(near.astype(BF), "y", -1), shift(far.astype(BF), "y", 1)
    grad_w = (gw[0] + near.astype(F32) + far.astype(F32)).reshape(r, n)
    return (proj_out, grad_attn, grad_w)


def solution(mesh):
    fine = Mesh(mesh.devices.reshape(4, 8, 4, 2), ("y", "z", "x", "c"))
    dp, head = XC, ("y", "z")
    return jax.shard_map(
        shards,
        mesh=fine,
        in_specs=(P(dp, head), P(head), P(head), P(head, dp), P(dp + head, None)),
        out_specs=(P(dp + head, None), P(dp, head), P(head, dp)),
        check_vma=False,
    )
```

```python
import jax
import jax.numpy as jnp
from jax import lax
from jax.experimental import pallas as pl
from jax.experimental.pallas import tpu as pltpu
from jax.sharding import Mesh, PartitionSpec as P

BF = jnp.bfloat16
F32 = jnp.float32
XC = ("x", "c")
FWD = 2**30
BWD = 2**36
VMEM = pl.BlockSpec(memory_space=pltpu.VMEM)
SMEM = pl.BlockSpec(memory_space=pltpu.SMEM)


def exchange(v, axes):
    return lax.all_to_all(v, axes, split_axis=0, concat_axis=0, tiled=False)


def shift(v, axis, s):
    n = lax.axis_size(axis)
    return lax.ppermute(v, axis, [(i, (i + s) % n) for i in range(n)])


def place(where, e, s, nx):
    return ((where[0] - s) & (nx - 1)) * 2 + (where[1] ^ e)


def forward(where, own, other, w0, w1, w2a, w2b, w3, out):
    nx, ty, _ = own.shape
    nz, _, j, n = out.shape
    r = w0.shape[0]
    half = r // 2
    for e, a in enumerate((own, other)):
        rows = a[...].reshape(nx * ty, a.shape[2])
        total = jnp.dot(rows[:, :r], w0[...], preferred_element_type=F32)
        total += jnp.dot(rows[:, r : 2 * r], w1[...], preferred_element_type=F32)
        total += jnp.dot(rows[:, 2 * r : 2 * r + half], w2a[...], preferred_element_type=F32)
        total += jnp.dot(rows[:, 2 * r + half : 3 * r], w2b[...], preferred_element_type=F32)
        total += jnp.dot(rows[:, 3 * r :], w3[...], preferred_element_type=F32)
        for s in range(nx):
            out[:, place(where, e, s, nx)] = total[s * ty : (s + 1) * ty].reshape(nz, j, n)


def backward(where, g, w0, w1, w2a, w2b, w3, own, other, g_rel, rows):
    n = g.shape[3]
    nx, ny, ty, r = own.shape
    half = r // 2
    for e in range(2):
        for x in range(nx):
            k = e * nx + x
            v = g[:, 2 * x + (where[1] ^ e)]
            rows[k * ty : (k + 1) * ty] = v.astype(F32).reshape(ty, n).astype(BF)
    for e in range(2):
        for s in range(nx):
            k = e * nx + s
            at = pl.multiple_of((e * nx + ((where[0] - s) & (nx - 1))) * ty, ty)
            g_rel[k * ty : (k + 1) * ty] = rows[pl.ds(at, ty)]
    across = (((1,), (1,)), ((), ()))
    for s, w in enumerate(((w0,), (w1,), (w2a, w2b), (w3,))):
        at = (where[2] - s) & (ny - 1)
        width = r // len(w)
        for i, part in enumerate(w):
            v = lax.dot_general(rows[...], part[...], across, preferred_element_type=F32)
            v = v.reshape(2, nx, ty, width)
            own[:, at, :, i * width : (i + 1) * width] = v[0]
            other[:, at, :, i * width : (i + 1) * width] = v[1].astype(BF)


def call(kernel, out_shape, *args, scratch=(), flops):
    return pl.pallas_call(
        kernel,
        out_shape=out_shape,
        in_specs=[SMEM] + [VMEM] * (len(args) - 1),
        out_specs=jax.tree.map(lambda _: VMEM, out_shape),
        scratch_shapes=scratch,
        cost_estimate=pl.CostEstimate(flops=flops, bytes_accessed=flops // 400, transcendentals=0),
        compiler_params=pltpu.CompilerParams(vmem_limit_bytes=32 * 1024 * 1024),
    )(*args)


def shards(attn_out, head_mask, gate_scale, w_out, grad_out):
    nx, ny, nz, nc = (lax.axis_size(a) for a in "xyzc")
    me = lax.axis_index("y")
    where = jnp.stack([lax.axis_index("x"), lax.axis_index("c"), me]).astype(jnp.int32)
    t, r = attn_out.shape
    j, d = grad_out.shape
    n = d // (nx * nc)
    ty = t // ny
    half = r // 2

    w1, w3 = shift(w_out, "y", 1), shift(w_out, "y", -1)
    g = exchange(grad_out.reshape(j, nx * nc, n).transpose(1, 0, 2), XC)

    gate_vals = head_mask.astype(F32) * gate_scale
    col_gate = jnp.repeat(gate_vals, r // gate_vals.shape[0])
    gated = (attn_out.astype(F32) * col_gate[None, :]).astype(BF).reshape(ny, ty, r)

    a = [lax.dynamic_index_in_dim(gated, (me + s) % ny, 0, keepdims=False) for s in range(ny)]
    a = [a[0]] + [shift(a[s], "y", s) for s in range(1, ny)]
    a = jnp.concatenate(a, axis=1)
    a, g, w1, w3 = lax.optimization_barrier((a, g, w1, w3))
    g = exchange(jnp.broadcast_to(g[None], (nz,) + g.shape), "z")
    a = jnp.stack([a] + [shift(a, "x", s) for s in range(1, nx)])
    w2a, w2b = shift(w1[:half], "y", 1), shift(w3[half:], "y", -1)
    other = shift(a, "c", 1)
    w = (w_out, w1, w2a, w2b, w3)

    part = call(
        forward, jax.ShapeDtypeStruct((nz, nx * nc, j, n), F32), where, a, other, *w,
        flops=FWD,
    )
    proj = lax.psum_scatter(part, "z", scatter_dimension=0, tiled=False).astype(BF)

    own, back, g_rel = call(
        backward,
        (
            jax.ShapeDtypeStruct((nx, ny, ty, r), F32),
            jax.ShapeDtypeStruct((nx, ny, ty, r), BF),
            jax.ShapeDtypeStruct((nx * nc * ty, n), BF),
        ),
        where, g, *w,
        scratch=[pltpu.VMEM((nx * nc * ty, n), BF)],
        flops=BWD,
    )
    mine = (own + shift(back, "c", 1).astype(F32)).astype(BF).reshape(nx * ny, ty, r)
    mine = exchange(mine, ("x", "y")).astype(F32).reshape(nx, t, r).sum(axis=0)
    grad_attn = (mine * col_gate[None, :]).astype(BF)

    a_rel = jnp.concatenate([a, other]).reshape(nx * nc * ty, ny * r)
    gw = lax.dot_general(a_rel, g_rel, (((0,), (0,)), ((), ())), preferred_element_type=F32)
    gw = gw.reshape(ny, 2, half, n)
    near = gw[1].at[0].add(shift(gw[2, 0].astype(BF), "y", -1).astype(F32))
    far = gw[3].at[1].add(shift(gw[2, 1].astype(BF), "y", 1).astype(F32))
    near, far = shift(near.astype(BF), "y", -1), shift(far.astype(BF), "y", 1)
    proj = exchange(proj, XC)
    near, far, proj = lax.optimization_barrier((near, far, proj))
    grad_w = (gw[0] + near.astype(F32) + far.astype(F32)).reshape(r, n)
    proj_out = proj.transpose(1, 0, 2).reshape(j, d)
    return (proj_out, grad_attn, grad_w)


def solution(mesh):
    fine = Mesh(mesh.devices.reshape(4, 8, 4, 2), ("y", "z", "x", "c"))
    dp, head = XC, ("y", "z")
    return jax.shard_map(
        shards,
        mesh=fine,
        in_specs=(P(dp, head), P(head), P(head), P(head, dp), P(dp + head, None)),
        out_specs=(P(dp + head, None), P(dp, head), P(head, dp)),
        check_vma=False,
    )
```

```python
import jax
import jax.numpy as jnp
from jax import lax
from jax.experimental import pallas as pl
from jax.experimental.pallas import tpu as pltpu
from jax.sharding import Mesh, PartitionSpec as P

BF = jnp.bfloat16
F32 = jnp.float32
XC = ("x", "c")
FWD = 2**30
BWD = 7 * 2**31
VMEM = pl.BlockSpec(memory_space=pltpu.VMEM)
SMEM = pl.BlockSpec(memory_space=pltpu.SMEM)


def exchange(v, axes):
    return lax.all_to_all(v, axes, split_axis=0, concat_axis=0, tiled=False)


def shift(v, axis, s):
    n = lax.axis_size(axis)
    return lax.ppermute(v, axis, [(i, (i + s) % n) for i in range(n)])


def place(where, e, s, nx):
    return ((where[0] - s) & (nx - 1)) * 2 + (where[1] ^ e)


def forward(where, own, other, w0, w1, w2a, w2b, w3, out):
    nx, ty, _ = own.shape
    nz, _, j, n = out.shape
    r = w0.shape[0]
    half = r // 2
    for e, a in enumerate((own, other)):
        rows = a[...].reshape(nx * ty, a.shape[2])
        total = jnp.dot(rows[:, :r], w0[...], preferred_element_type=F32)
        total += jnp.dot(rows[:, r : 2 * r], w1[...], preferred_element_type=F32)
        total += jnp.dot(rows[:, 2 * r : 2 * r + half], w2a[...], preferred_element_type=F32)
        total += jnp.dot(rows[:, 2 * r + half : 3 * r], w2b[...], preferred_element_type=F32)
        total += jnp.dot(rows[:, 3 * r :], w3[...], preferred_element_type=F32)
        for s in range(nx):
            out[:, place(where, e, s, nx)] = total[s * ty : (s + 1) * ty].reshape(nz, j, n)


def backward(where, g, w0, w1, w2a, w2b, w3, own, other, g_rel, rows):
    n = g.shape[3]
    nx, ny, ty, r = own.shape
    half = r // 2
    for e in range(2):
        for x in range(nx):
            k = e * nx + x
            v = g[:, 2 * x + (where[1] ^ e)]
            rows[k * ty : (k + 1) * ty] = v.astype(F32).reshape(ty, n).astype(BF)
    for e in range(2):
        for s in range(nx):
            k = e * nx + s
            at = pl.multiple_of((e * nx + ((where[0] - s) & (nx - 1))) * ty, ty)
            g_rel[k * ty : (k + 1) * ty] = rows[pl.ds(at, ty)]
    across = (((1,), (1,)), ((), ()))
    for s, w in enumerate(((w0,), (w1,), (w2a, w2b), (w3,))):
        at = (where[2] - s) & (ny - 1)
        width = r // len(w)
        for i, part in enumerate(w):
            v = lax.dot_general(rows[...], part[...], across, preferred_element_type=F32)
            v = v.reshape(2, nx, ty, width)
            own[:, at, :, i * width : (i + 1) * width] = v[0]
            other[:, at, :, i * width : (i + 1) * width] = v[1].astype(BF)


def call(kernel, out_shape, *args, scratch=(), flops):
    return pl.pallas_call(
        kernel,
        out_shape=out_shape,
        in_specs=[SMEM] + [VMEM] * (len(args) - 1),
        out_specs=jax.tree.map(lambda _: VMEM, out_shape),
        scratch_shapes=scratch,
        cost_estimate=pl.CostEstimate(flops=flops, bytes_accessed=flops // 400, transcendentals=0),
        compiler_params=pltpu.CompilerParams(vmem_limit_bytes=32 * 1024 * 1024),
    )(*args)


def shards(attn_out, head_mask, gate_scale, w_out, grad_out):
    nx, ny, nz, nc = (lax.axis_size(a) for a in "xyzc")
    me = lax.axis_index("y")
    where = jnp.stack([lax.axis_index("x"), lax.axis_index("c"), me]).astype(jnp.int32)
    t, r = attn_out.shape
    j, d = grad_out.shape
    n = d // (nx * nc)
    ty = t // ny
    half = r // 2

    w1, w3 = shift(w_out, "y", 1), shift(w_out, "y", -1)
    g = exchange(grad_out.reshape(j, nx * nc, n).transpose(1, 0, 2), XC)

    gate_vals = head_mask.astype(F32) * gate_scale
    col_gate = jnp.repeat(gate_vals, r // gate_vals.shape[0])
    gated = (attn_out.astype(F32) * col_gate[None, :]).astype(BF).reshape(ny, ty, r)

    a = [lax.dynamic_index_in_dim(gated, (me + s) % ny, 0, keepdims=False) for s in range(ny)]
    a = [a[0]] + [shift(a[s], "y", s) for s in range(1, ny)]
    a = jnp.concatenate(a, axis=1)
    a, g, w1, w3 = lax.optimization_barrier((a, g, w1, w3))
    g = exchange(jnp.broadcast_to(g[None], (nz,) + g.shape), "z")
    a = jnp.stack([a] + [shift(a, "x", s) for s in range(1, nx)])
    w2a, w2b = shift(w1[:half], "y", 1), shift(w3[half:], "y", -1)
    a, w2a, w2b = lax.optimization_barrier((a, w2a, w2b))
    other = shift(a, "c", 1)
    w = (w_out, w1, w2a, w2b, w3)

    part = call(
        forward, jax.ShapeDtypeStruct((nz, nx * nc, j, n), F32), where, a, other, *w,
        flops=FWD,
    )
    proj = lax.psum_scatter(part, "z", scatter_dimension=0, tiled=False).astype(BF)

    own, back, g_rel = call(
        backward,
        (
            jax.ShapeDtypeStruct((nx, ny, ty, r), F32),
            jax.ShapeDtypeStruct((nx, ny, ty, r), BF),
            jax.ShapeDtypeStruct((nx * nc * ty, n), BF),
        ),
        where, g, *w,
        scratch=[pltpu.VMEM((nx * nc * ty, n), BF)],
        flops=BWD,
    )
    mine = (own + shift(back, "c", 1).astype(F32)).astype(BF).reshape(nx * ny, ty, r)
    mine = exchange(mine, ("x", "y")).astype(F32).reshape(nx, t, r).sum(axis=0)
    grad_attn = (mine * col_gate[None, :]).astype(BF)

    a_rel = jnp.concatenate([a, other]).reshape(nx * nc * ty, ny * r)
    gw = lax.dot_general(a_rel, g_rel, (((0,), (0,)), ((), ())), preferred_element_type=F32)
    gw = gw.reshape(ny, 2, half, n)
    near = gw[1].at[0].add(shift(gw[2, 0].astype(BF), "y", -1).astype(F32))
    far = gw[3].at[1].add(shift(gw[2, 1].astype(BF), "y", 1).astype(F32))
    near, far = shift(near.astype(BF), "y", -1), shift(far.astype(BF), "y", 1)
    proj = exchange(proj, XC)
    near, far, proj = lax.optimization_barrier((near, far, proj))
    grad_w = (gw[0] + near.astype(F32) + far.astype(F32)).reshape(r, n)
    proj_out = proj.transpose(1, 0, 2).reshape(j, d)
    return (proj_out, grad_attn, grad_w)


def solution(mesh):
    fine = Mesh(mesh.devices.reshape(4, 8, 4, 2), ("y", "z", "x", "c"))
    dp, head = XC, ("y", "z")
    return jax.shard_map(
        shards,
        mesh=fine,
        in_specs=(P(dp, head), P(head), P(head), P(head, dp), P(dp + head, None)),
        out_specs=(P(dp + head, None), P(dp, head), P(head, dp)),
        check_vma=False,
    )
```

```python
import jax
import jax.numpy as jnp
from jax import lax
from jax.experimental import pallas as pl
from jax.experimental.pallas import tpu as pltpu
from jax.sharding import Mesh, PartitionSpec as P

BF = jnp.bfloat16
F32 = jnp.float32
XC = ("x", "c")
FWD = 2**30
BWD = 2**36
VMEM = pl.BlockSpec(memory_space=pltpu.VMEM)
SMEM = pl.BlockSpec(memory_space=pltpu.SMEM)


def exchange(v, axes):
    return lax.all_to_all(v, axes, split_axis=0, concat_axis=0, tiled=False)


def shift(v, axis, s):
    n = lax.axis_size(axis)
    return lax.ppermute(v, axis, [(i, (i + s) % n) for i in range(n)])


def place(where, e, s, nx):
    return ((where[0] - s) & (nx - 1)) * 2 + (where[1] ^ e)


def forward(where, own, other, w0, w1, w2a, w2b, w3, out):
    nx, ty, _ = own.shape
    nz, _, j, n = out.shape
    r = w0.shape[0]
    half = r // 2
    for e, a in enumerate((own, other)):
        rows = a[...].reshape(nx * ty, a.shape[2])
        total = jnp.dot(rows[:, :r], w0[...], preferred_element_type=F32)
        total += jnp.dot(rows[:, r : 2 * r], w1[...], preferred_element_type=F32)
        total += jnp.dot(rows[:, 2 * r : 2 * r + half], w2a[...], preferred_element_type=F32)
        total += jnp.dot(rows[:, 2 * r + half : 3 * r], w2b[...], preferred_element_type=F32)
        total += jnp.dot(rows[:, 3 * r :], w3[...], preferred_element_type=F32)
        for s in range(nx):
            out[:, place(where, e, s, nx)] = total[s * ty : (s + 1) * ty].reshape(nz, j, n).astype(BF)


def backward(where, g, w0, w1, w2a, w2b, w3, own, other, g_rel, rows):
    n = g.shape[3]
    nx, ny, ty, r = own.shape
    half = r // 2
    for e in range(2):
        for x in range(nx):
            k = e * nx + x
            v = g[:, 2 * x + (where[1] ^ e)]
            rows[k * ty : (k + 1) * ty] = v.astype(F32).reshape(ty, n).astype(BF)
    for e in range(2):
        for s in range(nx):
            k = e * nx + s
            at = pl.multiple_of((e * nx + ((where[0] - s) & (nx - 1))) * ty, ty)
            g_rel[k * ty : (k + 1) * ty] = rows[pl.ds(at, ty)]
    across = (((1,), (1,)), ((), ()))
    for s, w in enumerate(((w0,), (w1,), (w2a, w2b), (w3,))):
        at = (where[2] - s) & (ny - 1)
        width = r // len(w)
        for i, part in enumerate(w):
            v = lax.dot_general(rows[...], part[...], across, preferred_element_type=F32)
            v = v.reshape(2, nx, ty, width)
            own[:, at, :, i * width : (i + 1) * width] = v[0]
            other[:, at, :, i * width : (i + 1) * width] = v[1].astype(BF)


def call(kernel, out_shape, *args, scratch=(), flops):
    return pl.pallas_call(
        kernel,
        out_shape=out_shape,
        in_specs=[SMEM] + [VMEM] * (len(args) - 1),
        out_specs=jax.tree.map(lambda _: VMEM, out_shape),
        scratch_shapes=scratch,
        cost_estimate=pl.CostEstimate(flops=flops, bytes_accessed=flops // 400, transcendentals=0),
        compiler_params=pltpu.CompilerParams(vmem_limit_bytes=32 * 1024 * 1024),
    )(*args)


def shards(attn_out, head_mask, gate_scale, w_out, grad_out):
    nx, ny, nz, nc = (lax.axis_size(a) for a in "xyzc")
    me = lax.axis_index("y")
    where = jnp.stack([lax.axis_index("x"), lax.axis_index("c"), me]).astype(jnp.int32)
    t, r = attn_out.shape
    j, d = grad_out.shape
    n = d // (nx * nc)
    ty = t // ny
    half = r // 2

    w1, w3 = shift(w_out, "y", 1), shift(w_out, "y", -1)
    g = exchange(grad_out.reshape(j, nx * nc, n).transpose(1, 0, 2), XC)

    gate_vals = head_mask.astype(F32) * gate_scale
    col_gate = jnp.repeat(gate_vals, r // gate_vals.shape[0])
    gated = (attn_out.astype(F32) * col_gate[None, :]).astype(BF).reshape(ny, ty, r)

    a = [lax.dynamic_index_in_dim(gated, (me + s) % ny, 0, keepdims=False) for s in range(ny)]
    a = [a[0]] + [shift(a[s], "y", s) for s in range(1, ny)]
    a = jnp.concatenate(a, axis=1)
    a, g, w1, w3 = lax.optimization_barrier((a, g, w1, w3))
    g = lax.all_gather(g.reshape(nx * nc * j, n), "z", axis=0, tiled=True)
    g = g.reshape(nz, nx * nc, j, n)
    a = jnp.stack([a] + [shift(a, "x", s) for s in range(1, nx)])
    w2a, w2b = shift(w1[:half], "y", 1), shift(w3[half:], "y", -1)
    other = shift(a, "c", 1)
    w = (w_out, w1, w2a, w2b, w3)

    part = call(
        forward, jax.ShapeDtypeStruct((nz, nx * nc, j, n), BF), where, a, other, *w,
        flops=FWD,
    )
    proj = exchange(part, "z").astype(F32).sum(axis=0).astype(BF)

    own, back, g_rel = call(
        backward,
        (
            jax.ShapeDtypeStruct((nx, ny, ty, r), F32),
            jax.ShapeDtypeStruct((nx, ny, ty, r), BF),
            jax.ShapeDtypeStruct((nx * nc * ty, n), BF),
        ),
        where, g, *w,
        scratch=[pltpu.VMEM((nx * nc * ty, n), BF)],
        flops=BWD,
    )
    mine = (own + shift(back, "c", 1).astype(F32)).astype(BF).reshape(nx * ny, ty, r)
    mine = exchange(mine, ("x", "y")).astype(F32).reshape(nx, t, r).sum(axis=0)
    grad_attn = (mine * col_gate[None, :]).astype(BF)

    a_rel = jnp.concatenate([a, other]).reshape(nx * nc * ty, ny * r)
    gw = lax.dot_general(a_rel, g_rel, (((0,), (0,)), ((), ())), preferred_element_type=F32)
    gw = gw.reshape(ny, 2, half, n)
    near = gw[1].at[0].add(shift(gw[2, 0].astype(BF), "y", -1).astype(F32))
    far = gw[3].at[1].add(shift(gw[2, 1].astype(BF), "y", 1).astype(F32))
    near, far = shift(near.astype(BF), "y", -1), shift(far.astype(BF), "y", 1)
    proj = exchange(proj, XC)
    near, far, proj = lax.optimization_barrier((near, far, proj))
    grad_w = (gw[0] + near.astype(F32) + far.astype(F32)).reshape(r, n)
    proj_out = proj.transpose(1, 0, 2).reshape(j, d)
    return (proj_out, grad_attn, grad_w)


def solution(mesh):
    fine = Mesh(mesh.devices.reshape(4, 8, 4, 2), ("y", "z", "x", "c"))
    dp, head = XC, ("y", "z")
    return jax.shard_map(
        shards,
        mesh=fine,
        in_specs=(P(dp, head), P(head), P(head), P(head, dp), P(dp + head, None)),
        out_specs=(P(dp + head, None), P(dp, head), P(head, dp)),
        check_vma=False,
    )
```

```python
import jax
import jax.numpy as jnp
from jax import lax
from jax.experimental import pallas as pl
from jax.experimental.pallas import tpu as pltpu
from jax.sharding import Mesh, PartitionSpec as P

BF = jnp.bfloat16
F32 = jnp.float32
XC = ("x", "c")
FWD = 2**30
BWD = 2**34
VMEM = pl.BlockSpec(memory_space=pltpu.VMEM)
SMEM = pl.BlockSpec(memory_space=pltpu.SMEM)


def exchange(v, axes):
    return lax.all_to_all(v, axes, split_axis=0, concat_axis=0, tiled=False)


def shift(v, axis, s):
    n = lax.axis_size(axis)
    return lax.ppermute(v, axis, [(i, (i + s) % n) for i in range(n)])


def place(where, e, s, nx):
    return ((where[0] - s) & (nx - 1)) * 2 + (where[1] ^ e)


def forward(where, own, other, w0, w1, w2a, w2b, w3, out):
    nx, ty, _ = own.shape
    nz, _, j, n = out.shape
    r = w0.shape[0]
    half = r // 2
    for e, a in enumerate((own, other)):
        rows = a[...].reshape(nx * ty, a.shape[2])
        total = jnp.dot(rows[:, :r], w0[...], preferred_element_type=F32)
        total += jnp.dot(rows[:, r : 2 * r], w1[...], preferred_element_type=F32)
        total += jnp.dot(rows[:, 2 * r : 2 * r + half], w2a[...], preferred_element_type=F32)
        total += jnp.dot(rows[:, 2 * r + half : 3 * r], w2b[...], preferred_element_type=F32)
        total += jnp.dot(rows[:, 3 * r :], w3[...], preferred_element_type=F32)
        for s in range(nx):
            out[:, place(where, e, s, nx)] = total[s * ty : (s + 1) * ty].reshape(nz, j, n)


def backward(where, g, w0, w1, w2a, w2b, w3, own, other, g_rel, rows):
    n = g.shape[3]
    nx, ny, ty, r = own.shape
    half = r // 2
    for e in range(2):
        for x in range(nx):
            k = e * nx + x
            v = g[:, 2 * x + (where[1] ^ e)]
            rows[k * ty : (k + 1) * ty] = v.astype(F32).reshape(ty, n).astype(BF)
    for e in range(2):
        for s in range(nx):
            k = e * nx + s
            at = pl.multiple_of((e * nx + ((where[0] - s) & (nx - 1))) * ty, ty)
            g_rel[k * ty : (k + 1) * ty] = rows[pl.ds(at, ty)]
    across = (((1,), (1,)), ((), ()))
    for s, w in enumerate(((w0,), (w1,), (w2a, w2b), (w3,))):
        at = (where[2] - s) & (ny - 1)
        width = r // len(w)
        for i, part in enumerate(w):
            v = lax.dot_general(rows[...], part[...], across, preferred_element_type=F32)
            v = v.reshape(2, nx, ty, width)
            own[:, at, :, i * width : (i + 1) * width] = v[0]
            other[:, at, :, i * width : (i + 1) * width] = v[1].astype(BF)


def call(kernel, out_shape, *args, scratch=(), flops):
    return pl.pallas_call(
        kernel,
        out_shape=out_shape,
        in_specs=[SMEM] + [VMEM] * (len(args) - 1),
        out_specs=jax.tree.map(lambda _: VMEM, out_shape),
        scratch_shapes=scratch,
        cost_estimate=pl.CostEstimate(flops=flops, bytes_accessed=flops // 400, transcendentals=0),
        compiler_params=pltpu.CompilerParams(vmem_limit_bytes=32 * 1024 * 1024),
    )(*args)


def shards(attn_out, head_mask, gate_scale, w_out, grad_out):
    nx, ny, nz, nc = (lax.axis_size(a) for a in "xyzc")
    me = lax.axis_index("y")
    where = jnp.stack([lax.axis_index("x"), lax.axis_index("c"), me]).astype(jnp.int32)
    t, r = attn_out.shape
    j, d = grad_out.shape
    n = d // (nx * nc)
    ty = t // ny
    half = r // 2

    w1, w3 = shift(w_out, "y", 1), shift(w_out, "y", -1)
    g = exchange(grad_out.reshape(j, nx * nc, n).transpose(1, 0, 2), XC)

    gate_vals = head_mask.astype(F32) * gate_scale
    col_gate = jnp.repeat(gate_vals, r // gate_vals.shape[0])
    gated = (attn_out.astype(F32) * col_gate[None, :]).astype(BF).reshape(ny, ty, r)

    a = [lax.dynamic_index_in_dim(gated, (me + s) % ny, 0, keepdims=False) for s in range(ny)]
    a = [a[0]] + [shift(a[s], "y", s) for s in range(1, ny)]
    a = jnp.concatenate(a, axis=1)
    a, g, w1, w3 = lax.optimization_barrier((a, g, w1, w3))
    g = exchange(jnp.broadcast_to(g[None], (nz,) + g.shape), "z")
    a = jnp.stack([a] + [shift(a, "x", s) for s in range(1, nx)])
    w2a, w2b = shift(w1[:half], "y", 1), shift(w3[half:], "y", -1)
    other = shift(a, "c", 1)
    w = (w_out, w1, w2a, w2b, w3)

    part = call(
        forward, jax.ShapeDtypeStruct((nz, nx * nc, j, n), F32), where, a, other, *w,
        flops=FWD,
    )
    proj = lax.psum_scatter(part, "z", scatter_dimension=0, tiled=False).astype(BF)

    own, back, g_rel = call(
        backward,
        (
            jax.ShapeDtypeStruct((nx, ny, ty, r), F32),
            jax.ShapeDtypeStruct((nx, ny, ty, r), BF),
            jax.ShapeDtypeStruct((nx * nc * ty, n), BF),
        ),
        where, g, *w,
        scratch=[pltpu.VMEM((nx * nc * ty, n), BF)],
        flops=BWD,
    )
    mine = (own + shift(back, "c", 1).astype(F32)).astype(BF).reshape(nx * ny, ty, r)
    mine = exchange(mine, ("x", "y")).astype(F32).reshape(nx, t, r).sum(axis=0)
    grad_attn = (mine * col_gate[None, :]).astype(BF)

    a_rel = jnp.concatenate([a, other]).reshape(nx * nc * ty, ny * r)
    gw = lax.dot_general(a_rel, g_rel, (((0,), (0,)), ((), ())), preferred_element_type=F32)
    gw = gw.reshape(ny, 2, half, n)
    near = gw[1].at[0].add(shift(gw[2, 0].astype(BF), "y", -1).astype(F32))
    far = gw[3].at[1].add(shift(gw[2, 1].astype(BF), "y", 1).astype(F32))
    near, far = shift(near.astype(BF), "y", -1), shift(far.astype(BF), "y", 1)
    proj = exchange(proj, XC)
    near, far, proj = lax.optimization_barrier((near, far, proj))
    grad_w = (gw[0] + near.astype(F32) + far.astype(F32)).reshape(r, n)
    proj_out = proj.transpose(1, 0, 2).reshape(j, d)
    return (proj_out, grad_attn, grad_w)


def solution(mesh):
    fine = Mesh(mesh.devices.reshape(4, 8, 4, 2), ("y", "z", "x", "c"))
    dp, head = XC, ("y", "z")
    return jax.shard_map(
        shards,
        mesh=fine,
        in_specs=(P(dp, head), P(head), P(head), P(head, dp), P(dp + head, None)),
        out_specs=(P(dp + head, None), P(dp, head), P(head, dp)),
        check_vma=False,
    )
```

```python
import jax
import jax.numpy as jnp
from jax import lax
from jax.experimental import pallas as pl
from jax.experimental.pallas import tpu as pltpu
from jax.sharding import Mesh, PartitionSpec as P

BF = jnp.bfloat16
F32 = jnp.float32
XC = ("x", "c")
FWD = 2**30
BWD = 2**36
VMEM = pl.BlockSpec(memory_space=pltpu.VMEM)
SMEM = pl.BlockSpec(memory_space=pltpu.SMEM)


def exchange(v, axes):
    return lax.all_to_all(v, axes, split_axis=0, concat_axis=0, tiled=False)


def shift(v, axis, s):
    n = lax.axis_size(axis)
    return lax.ppermute(v, axis, [(i, (i + s) % n) for i in range(n)])


def place(where, e, s, nx):
    return ((where[0] - s) & (nx - 1)) * 2 + (where[1] ^ e)


def forward(where, own, other, w0, w1, w2a, w2b, w3, out):
    nx, ty, _ = own.shape
    nz, _, j, n = out.shape
    r = w0.shape[0]
    half = r // 2
    for e, a in enumerate((own, other)):
        rows = a[...].reshape(nx * ty, a.shape[2])
        total = jnp.dot(rows[:, :r], w0[...], preferred_element_type=F32)
        total += jnp.dot(rows[:, r : 2 * r], w1[...], preferred_element_type=F32)
        total += jnp.dot(rows[:, 2 * r : 2 * r + half], w2a[...], preferred_element_type=F32)
        total += jnp.dot(rows[:, 2 * r + half : 3 * r], w2b[...], preferred_element_type=F32)
        total += jnp.dot(rows[:, 3 * r :], w3[...], preferred_element_type=F32)
        for s in range(nx):
            out[:, place(where, e, s, nx)] = total[s * ty : (s + 1) * ty].reshape(nz, j, n)


def backward(where, g, w0, w1, w2a, w2b, w3, own, other, g_rel, rows):
    n = g.shape[3]
    nx, ny, ty, r = own.shape
    half = r // 2
    for e in range(2):
        for x in range(nx):
            k = e * nx + x
            v = g[:, 2 * x + (where[1] ^ e)]
            rows[k * ty : (k + 1) * ty] = v.astype(F32).reshape(ty, n).astype(BF)
    for e in range(2):
        for s in range(nx):
            k = e * nx + s
            at = pl.multiple_of((e * nx + ((where[0] - s) & (nx - 1))) * ty, ty)
            g_rel[k * ty : (k + 1) * ty] = rows[pl.ds(at, ty)]
    across = (((1,), (1,)), ((), ()))
    for s, w in enumerate(((w0,), (w1,), (w2a, w2b), (w3,))):
        at = (where[2] - s) & (ny - 1)
        width = r // len(w)
        for i, part in enumerate(w):
            v = lax.dot_general(rows[...], part[...], across, preferred_element_type=F32)
            v = v.reshape(2, nx, ty, width)
            own[:, at, :, i * width : (i + 1) * width] = v[0]
            other[:, at, :, i * width : (i + 1) * width] = v[1].astype(BF)


def call(kernel, out_shape, *args, scratch=(), flops):
    return pl.pallas_call(
        kernel,
        out_shape=out_shape,
        in_specs=[SMEM] + [VMEM] * (len(args) - 1),
        out_specs=jax.tree.map(lambda _: VMEM, out_shape),
        scratch_shapes=scratch,
        cost_estimate=pl.CostEstimate(flops=flops, bytes_accessed=flops // 400, transcendentals=0),
        compiler_params=pltpu.CompilerParams(vmem_limit_bytes=32 * 1024 * 1024),
    )(*args)


def shards(attn_out, head_mask, gate_scale, w_out, grad_out):
    nx, ny, nz, nc = (lax.axis_size(a) for a in "xyzc")
    me = lax.axis_index("y")
    where = jnp.stack([lax.axis_index("x"), lax.axis_index("c"), me]).astype(jnp.int32)
    t, r = attn_out.shape
    j, d = grad_out.shape
    n = d // (nx * nc)
    ty = t // ny
    half = r // 2

    w1, w3 = shift(w_out, "y", 1), shift(w_out, "y", -1)
    g = exchange(grad_out.reshape(j, nx * nc, n).transpose(1, 0, 2), XC)

    gate_vals = head_mask.astype(F32) * gate_scale
    col_gate = jnp.repeat(gate_vals, r // gate_vals.shape[0])
    gated = (attn_out.astype(F32) * col_gate[None, :]).astype(BF).reshape(ny, ty, r)

    a = [lax.dynamic_index_in_dim(gated, (me + s) % ny, 0, keepdims=False) for s in range(ny)]
    a = [a[0]] + [shift(a[s], "y", s) for s in range(1, ny)]
    a = jnp.concatenate(a, axis=1)
    a, g, w1, w3 = lax.optimization_barrier((a, g, w1, w3))
    g = exchange(jnp.broadcast_to(g[None], (nz,) + g.shape), "z")
    a = jnp.stack([a] + [shift(a, "x", s) for s in range(1, nx)])
    w2a, w2b = shift(w1[:half], "y", 1), shift(w3[half:], "y", -1)
    other = shift(a, "c", 1)
    w = (w_out, w1, w2a, w2b, w3)

    part = call(
        forward, jax.ShapeDtypeStruct((nz, nx * nc, j, n), F32), where, a, other, *w,
        flops=FWD,
    )
    proj = lax.psum_scatter(part, "z", scatter_dimension=0, tiled=False).astype(BF)

    own, back, g_rel = call(
        backward,
        (
            jax.ShapeDtypeStruct((nx, ny, ty, r), F32),
            jax.ShapeDtypeStruct((nx, ny, ty, r), BF),
            jax.ShapeDtypeStruct((nx * nc * ty, n), BF),
        ),
        where, g, *w,
        scratch=[pltpu.VMEM((nx * nc * ty, n), BF)],
        flops=BWD,
    )
    mine = (own + shift(back, "c", 1).astype(F32)).astype(BF).reshape(nx * ny, ty, r)
    mine = exchange(mine, ("x", "y")).astype(F32).reshape(nx, t, r).sum(axis=0)
    grad_attn = (mine * col_gate[None, :]).astype(BF)

    a_rel = jnp.concatenate([a, other]).reshape(nx * nc * ty, ny * r)
    gw = lax.dot_general(a_rel, g_rel, (((0,), (0,)), ((), ())), preferred_element_type=F32)
    gw = gw.reshape(ny, 2, half, n)
    near = gw[1].at[0].add(shift(gw[2, 0].astype(BF), "y", -1).astype(F32))
    far = gw[3].at[1].add(shift(gw[2, 1].astype(BF), "y", 1).astype(F32))
    near, far = shift(near.astype(BF), "y", -1), shift(far.astype(BF), "y", 1)
    near, far, proj = lax.optimization_barrier((near, far, proj))
    proj = exchange(proj, XC)
    grad_w = (gw[0] + near.astype(F32) + far.astype(F32)).reshape(r, n)
    proj_out = proj.transpose(1, 0, 2).reshape(j, d)
    return (proj_out, grad_attn, grad_w)


def solution(mesh):
    fine = Mesh(mesh.devices.reshape(4, 8, 4, 2), ("y", "z", "x", "c"))
    dp, head = XC, ("y", "z")
    return jax.shard_map(
        shards,
        mesh=fine,
        in_specs=(P(dp, head), P(head), P(head), P(head, dp), P(dp + head, None)),
        out_specs=(P(dp + head, None), P(dp, head), P(head, dp)),
        check_vma=False,
    )
```

```python
import jax
import jax.numpy as jnp
from jax import lax
from jax.experimental import pallas as pl
from jax.experimental.pallas import tpu as pltpu
from jax.sharding import Mesh, PartitionSpec as P

BF = jnp.bfloat16
F32 = jnp.float32
XC = ("x", "c")
FWD = 2**30
BWD = 2**34
VMEM = pl.BlockSpec(memory_space=pltpu.VMEM)
SMEM = pl.BlockSpec(memory_space=pltpu.SMEM)


def exchange(v, axes):
    return lax.all_to_all(v, axes, split_axis=0, concat_axis=0, tiled=False)


def shift(v, axis, s):
    n = lax.axis_size(axis)
    return lax.ppermute(v, axis, [(i, (i + s) % n) for i in range(n)])


def place(where, e, s, nx):
    return ((where[0] - s) & (nx - 1)) * 2 + (where[1] ^ e)


def forward(where, own, other, w0, w1a, w1b, w2a, w2b, w3a, w3b, out):
    nx, ty, _ = own.shape
    nz, _, j, n = out.shape
    r = w0.shape[0]
    half = r // 2
    for e, a in enumerate((own, other)):
        rows = a[...].reshape(nx * ty, a.shape[2])
        total = jnp.dot(rows[:, :r], w0[...], preferred_element_type=F32)
        for i, part in enumerate((w1a, w1b, w2a, w2b, w3a, w3b)):
            cols = slice(r + i * half, r + (i + 1) * half)
            total += jnp.dot(rows[:, cols], part[...], preferred_element_type=F32)
        for s in range(nx):
            out[:, place(where, e, s, nx)] = total[s * ty : (s + 1) * ty].reshape(nz, j, n)


def backward(where, g, w0, w1a, w1b, w2a, w2b, w3a, w3b, own, other, g_rel, rows):
    n = g.shape[3]
    nx, ny, ty, r = own.shape
    half = r // 2
    for e in range(2):
        for x in range(nx):
            k = e * nx + x
            v = g[:, 2 * x + (where[1] ^ e)]
            rows[k * ty : (k + 1) * ty] = v.astype(F32).reshape(ty, n).astype(BF)
    for e in range(2):
        for s in range(nx):
            k = e * nx + s
            at = pl.multiple_of((e * nx + ((where[0] - s) & (nx - 1))) * ty, ty)
            g_rel[k * ty : (k + 1) * ty] = rows[pl.ds(at, ty)]
    across = (((1,), (1,)), ((), ()))
    for s, w in enumerate(((w0,), (w1a, w1b), (w2a, w2b), (w3a, w3b))):
        at = (where[2] - s) & (ny - 1)
        width = r // len(w)
        for i, part in enumerate(w):
            v = lax.dot_general(rows[...], part[...], across, preferred_element_type=F32)
            v = v.reshape(2, nx, ty, width)
            own[:, at, :, i * width : (i + 1) * width] = v[0]
            other[:, at, :, i * width : (i + 1) * width] = v[1].astype(BF)


def call(kernel, out_shape, *args, scratch=(), flops):
    return pl.pallas_call(
        kernel,
        out_shape=out_shape,
        in_specs=[SMEM] + [VMEM] * (len(args) - 1),
        out_specs=jax.tree.map(lambda _: VMEM, out_shape),
        scratch_shapes=scratch,
        cost_estimate=pl.CostEstimate(flops=flops, bytes_accessed=flops // 400, transcendentals=0),
        compiler_params=pltpu.CompilerParams(vmem_limit_bytes=32 * 1024 * 1024),
    )(*args)


def shards(attn_out, head_mask, gate_scale, w_out, grad_out):
    nx, ny, nz, nc = (lax.axis_size(a) for a in "xyzc")
    me = lax.axis_index("y")
    where = jnp.stack([lax.axis_index("x"), lax.axis_index("c"), me]).astype(jnp.int32)
    t, r = attn_out.shape
    j, d = grad_out.shape
    n = d // (nx * nc)
    ty = t // ny
    half = r // 2

    w1a, w3b = shift(w_out[:half], "y", 1), shift(w_out[half:], "y", -1)
    w1b, w3a = shift(w_out[half:], "y", 1), shift(w_out[:half], "y", -1)
    w2a, w2b = shift(w1a, "y", 1), shift(w3b, "y", -1)
    g = exchange(grad_out.reshape(j, nx * nc, n).transpose(1, 0, 2), XC)

    gate_vals = head_mask.astype(F32) * gate_scale
    col_gate = jnp.repeat(gate_vals, r // gate_vals.shape[0])
    gated = (attn_out.astype(F32) * col_gate[None, :]).astype(BF).reshape(ny, ty, r)

    a = [lax.dynamic_index_in_dim(gated, (me + s) % ny, 0, keepdims=False) for s in range(ny)]
    a = [a[0]] + [shift(a[s], "y", s) for s in range(1, ny)]
    a = jnp.concatenate(a, axis=1)
    a, g, w2a, w2b, w1b, w3a = lax.optimization_barrier((a, g, w2a, w2b, w1b, w3a))
    g = exchange(jnp.broadcast_to(g[None], (nz,) + g.shape), "z")
    a = jnp.stack([a] + [shift(a, "x", s) for s in range(1, nx)])
    other = shift(a, "c", 1)
    w = (w_out, w1a, w1b, w2a, w2b, w3a, w3b)

    part = call(
        forward, jax.ShapeDtypeStruct((nz, nx * nc, j, n), F32), where, a, other, *w,
        flops=FWD,
    )
    proj = lax.psum_scatter(part, "z", scatter_dimension=0, tiled=False).astype(BF)

    own, back, g_rel = call(
        backward,
        (
            jax.ShapeDtypeStruct((nx, ny, ty, r), F32),
            jax.ShapeDtypeStruct((nx, ny, ty, r), BF),
            jax.ShapeDtypeStruct((nx * nc * ty, n), BF),
        ),
        where, g, *w,
        scratch=[pltpu.VMEM((nx * nc * ty, n), BF)],
        flops=BWD,
    )
    mine = (own + shift(back, "c", 1).astype(F32)).astype(BF).reshape(nx * ny, ty, r)
    mine = exchange(mine, ("x", "y")).astype(F32).reshape(nx, t, r).sum(axis=0)
    grad_attn = (mine * col_gate[None, :]).astype(BF)

    a_rel = jnp.concatenate([a, other]).reshape(nx * nc * ty, ny * r)
    gw = lax.dot_general(a_rel, g_rel, (((0,), (0,)), ((), ())), preferred_element_type=F32)
    gw = gw.reshape(ny, 2, half, n)
    near = gw[1].at[0].add(shift(gw[2, 0].astype(BF), "y", -1).astype(F32))
    far = gw[3].at[1].add(shift(gw[2, 1].astype(BF), "y", 1).astype(F32))
    near, far = shift(near.astype(BF), "y", -1), shift(far.astype(BF), "y", 1)
    proj = exchange(proj, XC)
    near, far, proj = lax.optimization_barrier((near, far, proj))
    grad_w = (gw[0] + near.astype(F32) + far.astype(F32)).reshape(r, n)
    proj_out = proj.transpose(1, 0, 2).reshape(j, d)
    return (proj_out, grad_attn, grad_w)


def solution(mesh):
    fine = Mesh(mesh.devices.reshape(4, 8, 4, 2), ("y", "z", "x", "c"))
    dp, head = XC, ("y", "z")
    return jax.shard_map(
        shards,
        mesh=fine,
        in_specs=(P(dp, head), P(head), P(head), P(head, dp), P(dp + head, None)),
        out_specs=(P(dp + head, None), P(dp, head), P(head, dp)),
        check_vma=False,
    )
```
